32 devices in a mesh: gx: 8 (over z, core), gy: 4 (over y, x).
Axes of the slice: x: 2, y: 2, z: 4, core: 2. Of those that a mesh axis runs over, the one named last changes fastest.
Arguments:
- tokens: bfloat16 [64, 32, 8, 768], P('gx', 'gy'), may hold values from -64 to 64
- target: bfloat16 [64, 32, 8, 768], P('gx', 'gy'), may hold values from -4 to 4
- norm_gain: float32 [768], replicated, may hold values from 0.1 to 1.9
- qkv_weight: bfloat16 [768, 1152], P('gy'), may hold values from -4 to 4
- proj_weight: bfloat16 [384, 768], P('gy'), may hold values from -1.5 to 1.5
Outputs:
- block_out: bfloat16 [64, 32, 8, 768], P('gx', 'gy')
- qkv_grad: float32 [768, 1152], P('gy')
The draws below stay inside these ranges and needn't reach their ends.
All inputs are finite; a program needn't handle non-finite values.
Results may differ from the reference program's by a relative error of at most 0.0094.
Values may be sent and summed in bfloat16 or wider, within the bound.
A program may use at most 64 MiB of HBM per device.

```python
import math
import jax
import jax.numpy as jnp
from jax import lax

D = 768
HEADS = 12
HD = 32
WIN = 8
INNER = 384
NX = 64
NY = 32
NZ = 8
TOKENS = 16384


def draw_tokens(key, part):
    base = jax.random.truncated_normal(key, -6.0, 6.0, (NX, NY, NZ, D), jnp.float32)
    return base.astype(jnp.bfloat16)


def draw_qkv_weight(key, part):
    weights = jax.random.truncated_normal(key, -6.0, 6.0, (D, 3 * INNER), jnp.float32) / jnp.sqrt(jnp.float32(D))
    return weights.astype(jnp.bfloat16)


def levels(rng, extent, pieces, low, high):
    def one(dim, shards_of):
        heights = jax.random.uniform(jax.random.fold_in(jax.random.fold_in(rng, 6), dim), (shards_of,), jnp.float32, low / len(pieces), high / len(pieces))
        return jnp.repeat(jnp.exp(heights), extent[dim] // shards_of).reshape((-1,) + (1,) * (len(extent) - dim - 1))

    level = one(*pieces[0])
    for cut in pieces[1:]:
        level = level * one(*cut)
    return level


def bell_draw(rng, extent, width, bound, pieces=(), held_as=jnp.bfloat16):
    gain = levels(rng, extent, pieces, -0.22, 0.18) if pieces else 1.0
    values = jax.random.normal(rng, extent, jnp.float32) * width * gain
    return jnp.minimum(jnp.maximum(values, -bound), bound).astype(held_as)


def setup_inputs(seed: int = 0) -> dict:
    splits = jax.random.split(jax.random.key(seed), 6)
    tokens = draw_tokens(jax.random.fold_in(splits[5], 71), 0)
    target = bell_draw(splits[1], (NX, NY, NZ, D), 0.5, 4.0, ((0, 8), (1, 4)))
    norm_gain = jnp.clip(1.0 + 0.18 * jax.random.normal(splits[2], (D,), jnp.float32), 0.1, 1.9)
    qkv_weight = draw_qkv_weight(jax.random.fold_in(splits[5], 71), 0)
    proj_weight = bell_draw(splits[4], (INNER, D), 16 ** -0.5, 1.5, ((0, 4),))
    return dict(tokens=tokens, target=target, norm_gain=norm_gain, qkv_weight=qkv_weight, proj_weight=proj_weight)


def narrow(values):
    return lax.optimization_barrier(values.astype(jnp.bfloat16)).astype(jnp.float32)

def layer_norm(tokens, norm_gain):
    widened = tokens.astype(jnp.float32)
    token_mean = lax.optimization_barrier(jnp.mean(widened, -1, keepdims=True))
    centred = widened - token_mean
    variance = lax.optimization_barrier(jnp.mean(centred * centred, -1, keepdims=True))
    return (centred * lax.rsqrt(variance + 1e-05) * norm_gain.astype(jnp.float32)).astype(jnp.bfloat16)

def into_windows(volume):
    ext_x, ext_y, ext_z, channels = volume.shape
    blocks = volume.reshape(ext_x // WIN, WIN, ext_y // WIN, WIN, ext_z // WIN, WIN, channels)
    return blocks.transpose(0, 2, 4, 1, 3, 5, 6).reshape(-1, WIN ** 3, channels)

def from_windows(windows, ext_x, ext_y, ext_z):
    channels = windows.shape[-1]
    blocks = windows.reshape(ext_x // WIN, ext_y // WIN, ext_z // WIN, WIN, WIN, WIN, channels)
    return blocks.transpose(0, 3, 1, 4, 2, 5, 6).reshape(ext_x, ext_y, ext_z, channels)

def split_heads(block):
    return block.astype(jnp.float32).reshape(block.shape[0], HEADS, HD)

def attention_probs(qkv_block):
    queries = split_heads(qkv_block[:, :INNER])
    keys_in = split_heads(qkv_block[:, INNER:2 * INNER])
    values = split_heads(qkv_block[:, 2 * INNER:])
    scores = jnp.einsum('qhd,khd->hqk', queries, keys_in) * HD ** (-0.5)
    row_max = lax.optimization_barrier(jnp.max(scores, -1, keepdims=True))
    exponent = jnp.exp(scores - row_max)
    probs = exponent / lax.optimization_barrier(jnp.sum(exponent, -1, keepdims=True))
    return (probs, queries, keys_in, values)

def window_forward(qkv_block):
    probs, queries, keys_in, values = attention_probs(qkv_block)
    mixed = jnp.einsum('hqk,khd->qhd', narrow(probs), values)
    return mixed.reshape(-1, INNER).astype(jnp.bfloat16)

def window_backward(inputs_pair):
    qkv_block, grad_block = inputs_pair
    probs, queries, keys_in, values = attention_probs(qkv_block)
    grad_mixed = split_heads(grad_block)
    grad_probs = jnp.einsum('qhd,khd->hqk', grad_mixed, values)
    grad_values = jnp.einsum('hqk,qhd->khd', narrow(probs), grad_mixed).astype(jnp.bfloat16)
    row_dot = lax.optimization_barrier(jnp.sum(grad_probs * probs, -1, keepdims=True))
    grad_scores = narrow(probs * (grad_probs - row_dot))
    grad_queries = (jnp.einsum('hqk,khd->qhd', grad_scores, keys_in) * HD ** (-0.5)).astype(jnp.bfloat16)
    grad_keys = (jnp.einsum('hqk,qhd->khd', grad_scores, queries) * HD ** (-0.5)).astype(jnp.bfloat16)
    return jnp.concatenate([grad_queries.reshape(-1, INNER), grad_keys.reshape(-1, INNER), grad_values.reshape(-1, INNER)], 1)

def reference(tokens, target, norm_gain, qkv_weight, proj_weight):
    half_width = WIN // 2
    normed = layer_norm(tokens, norm_gain)
    shifted = jnp.roll(normed, (-half_width, -half_width, -half_width), axis=(0, 1, 2))
    windows_in = into_windows(shifted)
    flat_in = windows_in.reshape(-1, D)
    qkv_act = jnp.dot(flat_in, qkv_weight, preferred_element_type=jnp.float32).astype(jnp.bfloat16)
    qkv_act = qkv_act.reshape(windows_in.shape[0], WIN ** 3, 3 * INNER)
    attn_out = lax.map(window_forward, qkv_act)
    block_shift = jnp.dot(attn_out.reshape(-1, INNER), proj_weight, preferred_element_type=jnp.float32).astype(jnp.bfloat16)
    block_vol = from_windows(block_shift.reshape(-1, WIN ** 3, D), NX, NY, NZ)
    block_out = jnp.roll(block_vol, (half_width, half_width, half_width), axis=(0, 1, 2))
    grad_out = ((block_out.astype(jnp.float32) - target.astype(jnp.float32)) * (2.0 / math.sqrt(TOKENS))).astype(jnp.bfloat16)
    grad_shift = into_windows(jnp.roll(grad_out, (-half_width, -half_width, -half_width), axis=(0, 1, 2)))
    grad_attn = jnp.dot(grad_shift.reshape(-1, D), proj_weight.T, preferred_element_type=jnp.float32).astype(jnp.bfloat16)
    grad_qkv = lax.map(window_backward, (qkv_act, grad_attn.reshape(-1, WIN ** 3, INNER)))
    qkv_grad = jnp.dot(flat_in.T, grad_qkv.reshape(-1, 3 * INNER), preferred_element_type=jnp.float32)
    return (block_out, qkv_grad)
```

```python
import functools
import math

import jax
import jax.numpy as jnp
from jax import lax
from jax.experimental import pallas as pl
from jax.experimental.pallas import tpu as pltpu
from jax.sharding import PartitionSpec as P

HEADS = 12
HD = 32
WIN = 8
HALF = WIN // 2
INNER = HEADS * HD
GROUPS = 3
GH = HEADS // GROUPS
GC = GH * HD
F32 = jnp.float32
BF16 = jnp.bfloat16
MESH = pl.DeviceIdType.MESH
norm_eps = 1e-05


def dot(a, b, ca, cb):
    return lax.dot_general(a, b, (((ca,), (cb,)), ((), ())), preferred_element_type=F32)


def flat_rows(x):
    rows = math.prod(x.shape[:-1])
    if x.shape[-2] % 16 == 0:
        return x.reshape(rows, x.shape[-1])
    return x.astype(F32).reshape(rows, x.shape[-1]).astype(BF16)


def kernel(
    nx, ny, scatter, loss_scale,
    tok, tgt, gain, wq, wp,
    out, grad,
    win, twin, wbuf, pbuf, xt, qkvt, ebuf, rinv, ot, blk, dot_t, dgrp,
    snd1, rcv1, s1, rcv2, snd3, rcv3, fin,
    ssem, rsem, lsem,
):
    nz = nx // 2
    x = lax.axis_index("gx")
    y = lax.axis_index("gy")
    core = lax.rem(x, 2)
    sib = x + 1 - 2 * core
    z = x // 2
    counter = [0]

    def gxi(d):
        return lax.rem(x + d + nx, nx)

    def gyi(d):
        return lax.rem(y + d + ny, ny)

    def remote(src, dst, dev):
        k = counter[0]
        counter[0] += 1
        return pltpu.make_async_remote_copy(
            src_ref=src, dst_ref=dst, send_sem=ssem.at[k], recv_sem=rsem.at[k],
            device_id=dev, device_id_type=MESH,
        )

    sent = []

    def go(copies):
        for c in copies:
            c.start()
            sent.append(c)

    peers = [(x, gyi(d)) for d in range(1, ny)]
    peers += [(gxi(1), y), (gxi(-1), y)]
    peers += [(gxi(2 * d), y) for d in range(1, nz)]
    peers += [(gxi(1), gyi(1)), (gxi(-1), gyi(-1))]
    barrier = pltpu.get_barrier_semaphore()
    for dev in peers:
        pl.semaphore_signal(barrier, inc=1, device_id=dev, device_id_type=MESH)
    locals_ = [
        pltpu.make_async_copy(tok.at[pl.ds(HALF, HALF), 1], win.at[0], lsem.at[0]),
        pltpu.make_async_copy(tgt.at[pl.ds(HALF, HALF), 1], twin.at[0], lsem.at[1]),
        pltpu.make_async_copy(wq, wbuf.at[y], lsem.at[2]),
        pltpu.make_async_copy(wp, pbuf.at[y], lsem.at[3]),
    ]
    for c in locals_:
        c.start()
    pl.semaphore_wait(barrier, len(peers))

    quarters = [(0, 1), (1, 0), (1, 1)]
    tok_copies = [
        remote(tok.at[pl.ds(HALF * (1 - a), HALF), 1 - b], win.at[2 * a + b], (gxi(-a), gyi(-b)))
        for a, b in quarters
    ]
    w_copies = [remote(wq.at[core], wbuf.at[y, core], (x, gyi(d))) for d in range(1, ny)]
    go(tok_copies)
    go(w_copies)

    def norm(q):
        v = win[q].reshape(-1, win.shape[-1]).astype(F32)
        mean = jnp.mean(v, -1, keepdims=True)
        cen = v - mean
        var = jnp.mean(cen * cen, -1, keepdims=True)
        nrm = cen * lax.rsqrt(var + norm_eps) * gain[...]
        rows = v.shape[0]
        xt[:, q * rows:(q + 1) * rows] = nrm.T.astype(BF16)

    locals_[0].wait()
    norm(0)
    w_fwd = []
    for d in range(1, ny):
        w_copies[d - 1].wait_recv()
        owner = gyi(-d)
        w_fwd.append(remote(wbuf.at[owner, core], wbuf.at[owner, core], (sib, y)))
        go(w_fwd[-1:])
    for (a, b), c in zip(quarters, tok_copies):
        c.wait_recv()
        norm(2 * a + b)
    p_copies = [remote(wp, pbuf.at[y], (x, gyi(d))) for d in range(1, ny)]
    t_copies = [
        remote(tgt.at[pl.ds(HALF * (1 - a), HALF), 1 - b], twin.at[2 * a + b], (gxi(-a), gyi(-b)))
        for a, b in quarters
    ]
    go(p_copies)
    go(t_copies)
    for c in w_fwd:
        c.wait_recv()
    locals_[2].wait()
    qkvt[...] = dot(flat_rows(wbuf[...]), xt[...], 0, 0).astype(BF16)

    scale = HD ** (-0.5)
    c2 = scale * math.log2(math.e)

    def rows_of(h, base=0):
        return pl.ds(pl.multiple_of(base + h * HD, HD), HD)

    def fwd(h, carry):
        q = qkvt[rows_of(h), :]
        k = qkvt[rows_of(h, INNER), :]
        v = qkvt[rows_of(h, 2 * INNER), :]
        s = dot(k, q, 0, 0)
        m = jnp.max(s, 0, keepdims=True)
        e = jnp.exp2((s - m) * c2)
        r = 1.0 / jnp.sum(e, 0, keepdims=True)
        eb = e.astype(BF16)
        ebuf[h] = eb
        rinv[h] = r
        ot[rows_of(h), :] = dot(v, eb, 1, 0) * r
        return carry

    lax.fori_loop(0, HEADS, fwd, 0)

    for c in p_copies:
        c.wait_recv()
    locals_[3].wait()
    proj = flat_rows(pbuf[...])
    res = dot(ot[...].astype(BF16), proj, 0, 0).astype(BF16)
    blk[...] = res.reshape(blk.shape)
    o_copies = [
        remote(blk.at[2 * a + b], out.at[pl.ds(HALF * (1 - a), HALF), 1 - b], (gxi(a), gyi(b)))
        for a, b in quarters
    ]
    go(o_copies)
    own = pltpu.make_async_copy(blk.at[0], out.at[pl.ds(HALF, HALF), 1], lsem.at[4])
    own.start()
    for c in t_copies:
        c.wait_recv()
    locals_[1].wait()
    tw = twin[...].reshape(res.shape)
    g = ((res.astype(F32) - tw.astype(F32)) * loss_scale).astype(BF16)
    dot_t[...] = dot(proj, g, 1, 1).astype(BF16)

    def bwd(h, g0):
        q = qkvt[rows_of(h), :]
        k = qkvt[rows_of(h, INNER), :]
        v = qkvt[rows_of(h, 2 * INNER), :]
        eb = ebuf[h]
        do = dot_t[rows_of(h), :].astype(F32) * rinv[h]
        dob = do.astype(BF16)
        rd = jnp.sum(do * ot[rows_of(h), :], 0, keepdims=True)
        dp = dot(v, dob, 0, 0)
        ds = (eb.astype(F32) * (dp - rd)).astype(BF16)
        hl = h - g0
        dgrp[rows_of(hl), :] = (dot(k, ds, 1, 0) * scale).astype(BF16)
        dgrp[rows_of(hl, GC), :] = (dot(q, ds, 1, 1) * scale).astype(BF16)
        dgrp[rows_of(hl, 2 * GC), :] = dot(dob, eb, 1, 1).astype(BF16)

    def half_group(i):
        per = GH // 2
        g0 = (i // 2) * GH

        def body(t, carry):
            bwd(i * per + t, g0)
            return carry

        lax.fori_loop(0, per, body, 0)

    st = {}

    def stage_a(i):
        dw = dot(xt[...], dgrp[...], 1, 1)
        hr = snd1.shape[3]
        dw = dw.reshape(ny, 2, hr, 3 * GC).astype(BF16)
        for cc in range(2):
            snd1[i, cc] = dw[:, cc]
        st["a", i] = [remote(snd1.at[i, 1 - core], rcv1.at[i], (sib, y))]
        go(st["a", i])

    def stage_b(i):
        for c in st["a", i]:
            c.wait_recv()
        s1[i] = (snd1[i, core].astype(F32) + rcv1[i].astype(F32)).astype(BF16)
        st["b", i] = [
            remote(s1.at[i, gyi(d)], rcv2.at[i, d - 1], (x, gyi(d))) for d in range(1, ny)
        ]
        go(st["b", i])

    def stage_c(i):
        acc = s1[i, y].astype(F32)
        for d in range(1, ny):
            st["b", i][d - 1].wait_recv()
            acc = acc + rcv2[i, d - 1].astype(F32)
        snd3[i] = acc.reshape(snd3.shape[1:]).astype(BF16)
        copies = []
        for d in range(1, nz):
            piece = lax.rem(z + d, nz) if scatter else 0
            copies.append(remote(snd3.at[i, piece], rcv3.at[i, d - 1], (gxi(2 * d), y)))
        st["c", i] = copies
        go(copies)

    def stage_d(i):
        piece = z if scatter else 0
        acc = snd3[i, piece].astype(F32)
        for d in range(1, nz):
            st["c", i][d - 1].wait_recv()
            acc = acc + rcv3[i, d - 1].astype(F32)
        fin[i, core, piece] = acc.astype(BF16)
        st["d", i] = []
        if scatter:
            st["d", i] = [
                remote(fin.at[i, core, z], fin.at[i, core, z], (gxi(2 * d), y))
                for d in range(1, nz)
            ]
            go(st["d", i])

    def stage_e(i):
        for c in st["d", i]:
            c.wait_recv()
        st["e", i] = [remote(fin.at[i, core], fin.at[i, core], (sib, y))]
        go(st["e", i])

    def stage_f(i):
        for c in st["e", i]:
            c.wait_recv()
        res = fin[i].astype(F32).reshape(grad.shape[0], 3 * GC)
        for part in range(3):
            lo = part * INNER + i * GC
            grad[:, lo:lo + GC] = res[:, part * GC:(part + 1) * GC]

    half_group(0)
    half_group(1)
    stage_a(0)
    half_group(2)
    stage_b(0)
    half_group(3)
    stage_a(1)
    stage_c(0)
    half_group(4)
    stage_b(1)
    half_group(5)
    stage_a(2)
    stage_d(0)
    stage_c(1)
    stage_b(2)
    stage_e(0)
    stage_d(1)
    stage_c(2)
    stage_f(0)
    stage_e(1)
    stage_d(2)
    stage_f(1)
    stage_e(2)
    stage_f(2)
    for c in o_copies:
        c.wait_recv()
    own.wait()
    for c in sent:
        c.wait_send()


def shards(nx, ny, tokens, target, norm_gain, qkv_weight, proj_weight):
    ex, ey, ez, ch = tokens.shape
    rows = HALF * ez
    wr = qkv_weight.shape[0]
    pr = proj_weight.shape[0]
    hr = wr // 2
    nz = nx // 2
    scatter = hr % (8 * nz) == 0
    pieces = nz if scatter else 1
    prow = hr // pieces
    n_tok = ex * ey * ez
    inner3 = qkv_weight.shape[1]
    gw = inner3 // GROUPS
    loss_scale = 2.0 / math.sqrt(n_tok * nx * ny)
    ncopies = 9 + 3 * (ny - 1) + GROUPS * (2 + (ny - 1) + (nz - 1) * (2 if scatter else 1))
    any_spec = pl.BlockSpec(memory_space=pl.ANY)
    vm_spec = pl.BlockSpec(memory_space=pltpu.VMEM)
    block, grad = pl.pallas_call(
        functools.partial(kernel, nx, ny, scatter, loss_scale),
        out_shape=(
            jax.ShapeDtypeStruct((ex, 2, rows, ch), BF16),
            jax.ShapeDtypeStruct((wr, inner3), F32),
        ),
        in_specs=[any_spec, any_spec, vm_spec, any_spec, any_spec],
        out_specs=(any_spec, vm_spec),
        scratch_shapes=[
            pltpu.VMEM((4, HALF, rows, ch), BF16),
            pltpu.VMEM((4, HALF, rows, ch), BF16),
            pltpu.VMEM((ny, 2, hr, inner3), BF16),
            pltpu.VMEM((ny, pr, ch), BF16),
            pltpu.VMEM((ch, n_tok), BF16),
            pltpu.VMEM((inner3, n_tok), BF16),
            pltpu.VMEM((HEADS, n_tok, n_tok), BF16),
            pltpu.VMEM((HEADS, 1, n_tok), F32),
            pltpu.VMEM((INNER, n_tok), F32),
            pltpu.VMEM((4, HALF, rows, ch), BF16),
            pltpu.VMEM((INNER, n_tok), BF16),
            pltpu.VMEM((gw, n_tok), BF16),
            pltpu.VMEM((GROUPS, 2, ny, hr, gw), BF16),
            pltpu.VMEM((GROUPS, ny, hr, gw), BF16),
            pltpu.VMEM((GROUPS, ny, hr, gw), BF16),
            pltpu.VMEM((GROUPS, ny - 1, hr, gw), BF16),
            pltpu.VMEM((GROUPS, pieces, prow, gw), BF16),
            pltpu.VMEM((GROUPS, nz - 1, prow, gw), BF16),
            pltpu.VMEM((GROUPS, 2, pieces, prow, gw), BF16),
            pltpu.SemaphoreType.DMA((ncopies,)),
            pltpu.SemaphoreType.DMA((ncopies,)),
            pltpu.SemaphoreType.DMA((5,)),
        ],
        compiler_params=pltpu.CompilerParams(
            collective_id=0, has_side_effects=True, vmem_limit_bytes=60 * 2**20
        ),
        name="step",
    )(
        tokens.reshape(ex, 2, rows, ch),
        target.reshape(ex, 2, rows, ch),
        norm_gain.reshape(1, ch),
        qkv_weight.reshape(2, hr, inner3),
        proj_weight,
    )
    return block.reshape(ex, ey, ez, ch), grad


def solution(mesh):
    nx, ny = mesh.shape["gx"], mesh.shape["gy"]
    in_specs = (
        P("gx", "gy", None, None),
        P("gx", "gy", None, None),
        P(),
        P("gy", None),
        P("gy", None),
    )
    out_specs = (P("gx", "gy", None, None), P("gy", None))
    return jax.shard_map(
        functools.partial(shards, nx, ny),
        mesh=mesh, in_specs=in_specs, out_specs=out_specs, check_vma=False,
    )
```

```python
import functools
import math

import jax
import jax.numpy as jnp
from jax import lax
from jax.experimental import pallas as pl
from jax.experimental.pallas import tpu as pltpu
from jax.sharding import PartitionSpec as P

HEADS = 12
HD = 32
WIN = 8
HALF = WIN // 2
INNER = HEADS * HD
GROUPS = 3
GH = HEADS // GROUPS
GC = GH * HD
F32 = jnp.float32
BF16 = jnp.bfloat16
MESH = pl.DeviceIdType.MESH
norm_eps = 1e-05


def dot(a, b, ca, cb):
    return lax.dot_general(a, b, (((ca,), (cb,)), ((), ())), preferred_element_type=F32)


def flat_rows(x):
    rows = math.prod(x.shape[:-1])
    if x.shape[-2] % 16 == 0:
        return x.reshape(rows, x.shape[-1])
    return x.astype(F32).reshape(rows, x.shape[-1]).astype(BF16)


def kernel(
    nx, ny, scatter, wsplit, psplit, loss_scale,
    tok, tgt, gain, wq, wp,
    out, grad,
    win, thome, tph, tpw, aw, ah, wbuf, pbuf, xt, qkvt, ebuf, rinv, ot, dot_t, dgrp,
    snd1, rcv1, s1, rcv2, snd3, rcv3, fin,
    ssem, rsem, lsem,
):
    nz = nx // 2
    x = lax.axis_index("gx")
    y = lax.axis_index("gy")
    core = lax.rem(x, 2)
    sib = x + 1 - 2 * core
    z = x // 2
    zodd = lax.rem(z, 2)
    zmate = x + 2 - 4 * zodd
    wpart = core + 2 * zodd if wsplit == 4 else core
    zpart = core + 2 * (1 - zodd)
    ppart = core if psplit == 2 else 0
    counter = [0]

    def gxi(d):
        return lax.rem(x + d + nx, nx)

    def gyi(d):
        return lax.rem(y + d + ny, ny)

    def remote(src, dst, dev):
        k = counter[0]
        counter[0] += 1
        return pltpu.make_async_remote_copy(
            src_ref=src, dst_ref=dst, send_sem=ssem.at[k], recv_sem=rsem.at[k],
            device_id=dev, device_id_type=MESH,
        )

    sent = []

    def go(copies):
        for c in copies:
            c.start()
            sent.append(c)

    peers = [(x, gyi(d)) for d in range(1, ny)]
    peers += [(gxi(1), y), (gxi(-1), y)]
    peers += [(gxi(2 * d), y) for d in range(1, nz)]
    peers += [(gxi(1), gyi(1)), (gxi(-1), gyi(-1))]
    barrier = pltpu.get_barrier_semaphore()
    for dev in peers:
        pl.semaphore_signal(barrier, inc=1, device_id=dev, device_id_type=MESH)
    locals_ = [
        pltpu.make_async_copy(tok.at[pl.ds(HALF, HALF), 1], win.at[0], lsem.at[0]),
        pltpu.make_async_copy(tgt, thome, lsem.at[1]),
        pltpu.make_async_copy(wq, wbuf.at[y], lsem.at[2]),
        pltpu.make_async_copy(wp, pbuf.at[y], lsem.at[3]),
    ]
    for c in locals_:
        c.start()
    pl.semaphore_wait(barrier, len(peers))

    quarters = [(0, 1), (1, 0), (1, 1)]
    tok_copies = [
        remote(tok.at[pl.ds(HALF * (1 - a), HALF), 1 - b], win.at[2 * a + b], (gxi(-a), gyi(-b)))
        for a, b in quarters
    ]
    w_copies = [remote(wq.at[wpart], wbuf.at[y, wpart], (x, gyi(d))) for d in range(1, ny)]
    p_copies = [remote(wp.at[ppart], pbuf.at[y, ppart], (x, gyi(d))) for d in range(1, ny)]
    go(w_copies)
    go(tok_copies)
    go(p_copies)

    def norm(q):
        v = win[q].reshape(-1, win.shape[-1]).astype(F32)
        mean = jnp.mean(v, -1, keepdims=True)
        cen = v - mean
        var = jnp.mean(cen * cen, -1, keepdims=True)
        nrm = cen * lax.rsqrt(var + norm_eps) * gain[...].reshape(1, -1)
        rows = v.shape[0]
        xt[:, q * rows:(q + 1) * rows] = nrm.T.astype(BF16)

    locals_[0].wait()
    norm(0)
    w_sib = []
    w_z = []
    for d in range(1, ny):
        w_copies[d - 1].wait_recv()
        mine = wbuf.at[gyi(-d), wpart]
        if wsplit == 4:
            w_z.append(remote(mine, mine, (zmate, y)))
            go(w_z[-1:])
        w_sib.append(remote(mine, mine, (sib, y)))
        go(w_sib[-1:])
    order = [1, 0, 2]
    for t in order[:1]:
        tok_copies[t].wait_recv()
        norm(t + 1)
    for d in range(1, ny):
        if wsplit == 4:
            w_z[d - 1].wait_recv()
            other = wbuf.at[gyi(-d), zpart]
            w_sib.append(remote(other, other, (sib, y)))
            go(w_sib[-1:])
    for t in order[1:]:
        tok_copies[t].wait_recv()
        norm(t + 1)
    for c in w_sib:
        c.wait_recv()
    locals_[2].wait()
    qkvt[...] = dot(flat_rows(wbuf[...]), xt[...], 0, 0).astype(BF16)

    scale = HD ** (-0.5)
    c2 = scale * math.log2(math.e)

    def rows_of(h, base=0):
        return pl.ds(pl.multiple_of(base + h * HD, HD), HD)

    def fwd(h, carry):
        q = qkvt[rows_of(h), :]
        k = qkvt[rows_of(h, INNER), :]
        v = qkvt[rows_of(h, 2 * INNER), :]
        s = dot(k, q, 0, 0)
        m = jnp.max(s, 0, keepdims=True)
        e = jnp.exp2((s - m) * c2)
        r = 1.0 / jnp.sum(e, 0, keepdims=True)
        eb = e.astype(BF16)
        ebuf[h] = eb
        rinv[h] = r
        ot[rows_of(h), :] = dot(v, eb, 1, 0) * r
        return carry

    p_sib = []
    for d in range(1, ny):
        p_copies[d - 1].wait_recv()
        if psplit == 2:
            mine = pbuf.at[gyi(-d), ppart]
            p_sib.append(remote(mine, mine, (sib, y)))
            go(p_sib[-1:])
    lax.fori_loop(0, GH // 2, fwd, 0)
    for c in p_sib:
        c.wait_recv()
    locals_[3].wait()
    locals_[1].wait()
    proj = flat_rows(pbuf[...])
    n_tok = xt.shape[1]
    tph[...] = dot(thome[...].reshape(n_tok, -1), proj, 1, 1).astype(BF16).reshape(tph.shape)
    t_copies = [
        remote(tph.at[pl.ds(HALF * (1 - a), HALF), 1 - b], tpw.at[2 * a + b], (gxi(-a), gyi(-b)))
        for a, b in quarters
    ]
    go(t_copies)
    own_t = pltpu.make_async_copy(tph.at[pl.ds(HALF, HALF), 1], tpw.at[0], lsem.at[4])
    own_t.start()
    lax.fori_loop(GH // 2, HEADS, fwd, 0)

    attn = ot[...].T.astype(BF16)
    aw[...] = attn.reshape(aw.shape)
    o_copies = [
        remote(aw.at[2 * a + b], ah.at[pl.ds(HALF * (1 - a), HALF), 1 - b], (gxi(a), gyi(b)))
        for a, b in quarters
    ]
    go(o_copies)
    own_a = pltpu.make_async_copy(aw.at[0], ah.at[pl.ds(HALF, HALF), 1], lsem.at[5])
    own_a.start()
    proj = flat_rows(pbuf[...])
    res = dot(attn, proj, 1, 0).astype(BF16)
    back = dot(res, proj, 1, 1)
    for c in t_copies:
        c.wait_recv()
    own_t.wait()
    tw = tpw[...].reshape(n_tok, -1).astype(F32)
    dot_t[...] = ((back - tw) * loss_scale).T.astype(BF16)

    def bwd(h, g0):
        q = qkvt[rows_of(h), :]
        k = qkvt[rows_of(h, INNER), :]
        v = qkvt[rows_of(h, 2 * INNER), :]
        eb = ebuf[h]
        do = dot_t[rows_of(h), :].astype(F32) * rinv[h]
        dob = do.astype(BF16)
        rd = jnp.sum(do * ot[rows_of(h), :], 0, keepdims=True)
        dp = dot(v, dob, 0, 0)
        ds = (eb.astype(F32) * (dp - rd)).astype(BF16)
        hl = h - g0
        dgrp[rows_of(hl), :] = (dot(k, ds, 1, 0) * scale).astype(BF16)
        dgrp[rows_of(hl, GC), :] = (dot(q, ds, 1, 1) * scale).astype(BF16)
        dgrp[rows_of(hl, 2 * GC), :] = dot(dob, eb, 1, 1).astype(BF16)

    def half_group(i):
        per = GH // 2
        g0 = (i // 2) * GH

        def body(t, carry):
            bwd(i * per + t, g0)
            return carry

        lax.fori_loop(0, per, body, 0)

    st = {}

    def stage_a(i):
        dw = dot(xt[...], dgrp[...], 1, 1)
        hr = snd1.shape[3]
        dw = dw.reshape(ny, 2, hr, 3 * GC).astype(BF16)
        for cc in range(2):
            snd1[i, cc] = dw[:, cc]
        st["a", i] = [remote(snd1.at[i, 1 - core], rcv1.at[i], (sib, y))]
        go(st["a", i])

    def stage_b(i):
        for c in st["a", i]:
            c.wait_recv()
        s1[i] = (snd1[i, core].astype(F32) + rcv1[i].astype(F32)).astype(BF16)
        st["b", i] = [
            remote(s1.at[i, gyi(d)], rcv2.at[i, d - 1], (x, gyi(d))) for d in range(1, ny)
        ]
        go(st["b", i])

    def stage_c(i):
        acc = s1[i, y].astype(F32)
        for d in range(1, ny):
            st["b", i][d - 1].wait_recv()
            acc = acc + rcv2[i, d - 1].astype(F32)
        snd3[i] = acc.reshape(snd3.shape[1:]).astype(BF16)
        copies = []
        for d in range(1, nz):
            piece = lax.rem(z + d, nz) if scatter else 0
            copies.append(remote(snd3.at[i, piece], rcv3.at[i, d - 1], (gxi(2 * d), y)))
        st["c", i] = copies
        go(copies)

    def stage_d(i):
        piece = z if scatter else 0
        acc = snd3[i, piece].astype(F32)
        for d in range(1, nz):
            st["c", i][d - 1].wait_recv()
            acc = acc + rcv3[i, d - 1].astype(F32)
        fin[i, core, piece] = acc.astype(BF16)
        st["d", i] = []
        if scatter:
            st["d", i] = [
                remote(fin.at[i, core, z], fin.at[i, core, z], (gxi(2 * d), y))
                for d in range(1, nz)
            ]
            go(st["d", i])

    def stage_e(i):
        for c in st["d", i]:
            c.wait_recv()
        st["e", i] = [remote(fin.at[i, core], fin.at[i, core], (sib, y))]
        go(st["e", i])

    def stage_f(i):
        for c in st["e", i]:
            c.wait_recv()
        res = flat_rows(fin[i])
        for part in range(3):
            lo = part * INNER + i * GC
            grad[:, lo:lo + GC] = res[:, part * GC:(part + 1) * GC]

    half_group(0)
    half_group(1)
    stage_a(0)
    half_group(2)
    stage_b(0)
    half_group(3)
    stage_a(1)
    stage_c(0)
    half_group(4)
    stage_b(1)
    half_group(5)
    stage_a(2)
    stage_d(0)
    stage_c(1)
    for c in o_copies:
        c.wait_recv()
    own_a.wait()
    home = ah[...].reshape(n_tok, -1)
    out[...] = dot(home, flat_rows(pbuf[...]), 1, 0).astype(BF16)
    stage_b(2)
    stage_e(0)
    stage_d(1)
    stage_c(2)
    stage_f(0)
    stage_e(1)
    stage_d(2)
    stage_f(1)
    stage_e(2)
    stage_f(2)
    for c in sent:
        c.wait_send()


def finish(b_in, g_in, b_out, g_out):
    b_out[...] = b_in[...]
    g_out[...] = g_in[...].astype(F32)


def shards(nx, ny, tokens, target, norm_gain, qkv_weight, proj_weight):
    ex, ey, ez, ch = tokens.shape
    rows = HALF * ez
    wr = qkv_weight.shape[0]
    pr = proj_weight.shape[0]
    wsplit = 4 if wr % 64 == 0 else 2
    psplit = 2 if pr % 32 == 0 else 1
    hr = wr // 2
    nz = nx // 2
    scatter = hr % (8 * nz) == 0
    pieces = nz if scatter else 1
    prow = hr // pieces
    n_tok = ex * ey * ez
    inner3 = qkv_weight.shape[1]
    gw = inner3 // GROUPS
    loss_scale = 2.0 / math.sqrt(n_tok * nx * ny)
    ncopies = 9 + 6 * (ny - 1) + GROUPS * (2 + (ny - 1) + (nz - 1) * (2 if scatter else 1))
    any_spec = pl.BlockSpec(memory_space=pl.ANY)
    vm_spec = pl.BlockSpec(memory_space=pltpu.VMEM)
    block, grad = pl.pallas_call(
        functools.partial(kernel, nx, ny, scatter, wsplit, psplit, loss_scale),
        out_shape=(
            jax.ShapeDtypeStruct((n_tok, ch), BF16),
            jax.ShapeDtypeStruct((wr, inner3), BF16),
        ),
        in_specs=[any_spec, any_spec, vm_spec, any_spec, any_spec],
        out_specs=(vm_spec, vm_spec),
        scratch_shapes=[
            pltpu.VMEM((4, HALF, rows, ch), BF16),
            pltpu.VMEM((ex, 2, rows, ch), BF16),
            pltpu.VMEM((ex, 2, rows, INNER), BF16),
            pltpu.VMEM((4, HALF, rows, INNER), BF16),
            pltpu.VMEM((4, HALF, rows, INNER), BF16),
            pltpu.VMEM((ex, 2, rows, INNER), BF16),
            pltpu.VMEM((ny, wsplit, wr // wsplit, inner3), BF16),
            pltpu.VMEM((ny, psplit, pr // psplit, ch), BF16),
            pltpu.VMEM((ch, n_tok), BF16),
            pltpu.VMEM((inner3, n_tok), BF16),
            pltpu.VMEM((HEADS, n_tok, n_tok), BF16),
            pltpu.VMEM((HEADS, 1, n_tok), F32),
            pltpu.VMEM((INNER, n_tok), F32),
            pltpu.VMEM((INNER, n_tok), BF16),
            pltpu.VMEM((gw, n_tok), BF16),
            pltpu.VMEM((GROUPS, 2, ny, hr, gw), BF16),
            pltpu.VMEM((GROUPS, ny, hr, gw), BF16),
            pltpu.VMEM((GROUPS, ny, hr, gw), BF16),
            pltpu.VMEM((GROUPS, ny - 1, hr, gw), BF16),
            pltpu.VMEM((GROUPS, pieces, prow, gw), BF16),
            pltpu.VMEM((GROUPS, nz - 1, prow, gw), BF16),
            pltpu.VMEM((GROUPS, 2, pieces, prow, gw), BF16),
            pltpu.SemaphoreType.DMA((ncopies,)),
            pltpu.SemaphoreType.DMA((ncopies,)),
            pltpu.SemaphoreType.DMA((6,)),
        ],
        compiler_params=pltpu.CompilerParams(
            collective_id=0, has_side_effects=True, vmem_limit_bytes=60 * 2**20
        ),
        name="step",
    )(
        tokens.reshape(ex, 2, rows, ch),
        target.reshape(ex, 2, rows, ch),
        norm_gain,
        qkv_weight.reshape(wsplit, wr // wsplit, inner3),
        proj_weight.reshape(psplit, pr // psplit, ch),
    )
    steps = 4 if wr % 64 == 0 else 1
    bspec = pl.BlockSpec((n_tok // steps, ch), lambda i: (i, 0))
    gspec = pl.BlockSpec((wr // steps, inner3), lambda i: (i, 0))
    block, grad = pl.pallas_call(
        finish,
        grid=(steps,),
        out_shape=(
            jax.ShapeDtypeStruct(block.shape, BF16),
            jax.ShapeDtypeStruct(grad.shape, F32),
        ),
        in_specs=[bspec, gspec],
        out_specs=(bspec, gspec),
        name="finish",
    )(block, grad)
    return block.reshape(ex, ey, ez, ch), grad


def solution(mesh):
    nx, ny = mesh.shape["gx"], mesh.shape["gy"]
    in_specs = (
        P("gx", "gy", None, None),
        P("gx", "gy", None, None),
        P(),
        P("gy", None),
        P("gy", None),
    )
    out_specs = (P("gx", "gy", None, None), P("gy", None))
    return jax.shard_map(
        functools.partial(shards, nx, ny),
        mesh=mesh, in_specs=in_specs, out_specs=out_specs, check_vma=False,
    )
```
